32 devices in a mesh: groups: 2 (over x), hist: 16 (over z, y, core).
Axes of the slice: x: 2, y: 2, z: 4, core: 2. Of those that a mesh axis runs over, the one named last changes fastest.
Arguments:
- history: bfloat16 [16384, 1024], P(('groups', 'hist')), parts along dimension 0, may hold values from -6 to 6
- candidates: bfloat16 [512, 1024], P(('groups', 'hist')), parts along dimension 0, may hold values from -6 to 6
- hist_length: int32 [2], P('groups'), parts along dimension 0, may hold values from 4096 to 8192
- visible: int32 [512], P(('groups', 'hist')), parts along dimension 0, may hold values from 1 to 8192
- w_proj: bfloat16 [1024, 4096], replicated, may hold values from -0.1875 to 0.1875
- w_out: bfloat16 [1024, 1024], replicated, may hold values from -0.1875 to 0.1875
Outputs:
- scored: bfloat16 [512, 1024], P(('groups', 'hist')), parts along dimension 0
The draws below stay inside these ranges and needn't reach their ends.
There are 2 independent parts, one for each index of `groups`. The reference program is written for one: setup_inputs(seed, part) draws one part's arguments, and reference() takes and returns one part's arrays. A program takes and returns all parts, laid end to end along the dimension named above; an argument that names none is the same for every part. Nothing has to cross between parts.
All inputs are finite; a program needn't handle non-finite values.
Results may differ from the reference program's by a relative error of at most 0.0022.
The reference program's roundings to bfloat16 on the way (of `hist_norm`, `hist_kv`, `cand_norm`, `proj`, `weight` and `mixed`) count: a program that leaves them out, or rounds other values in their place, can miss the bound.
Values may be sent and summed in bfloat16 or wider, within the bound.
A program may use at most 64 MiB of HBM per device.

```python
import jax
import jax.numpy as jnp
from jax import lax

D = 1024
HEADS = 8
C_DEV = 16
HIST = 8192
NC = 256


def set_ends(values, own_key, low, high):
    longest = values.shape.index(max(values.shape))
    spots = []
    for shift in (0, 1):
        where = [jax.random.randint(jax.random.fold_in(own_key, axis), (), 0, length) for axis, length in enumerate(values.shape)]
        where[longest] = (where[longest] + shift) % values.shape[longest]
        spots.append(tuple(where))
    return values.at[spots[0]].set(low).at[spots[1]].set(high)


def steps_of(stream_key, shape, shards, low, top_value):
    factor_of = 1.0
    for dim, parts in shards:
        steps = jax.random.uniform(jax.random.fold_in(jax.random.fold_in(stream_key, 6), dim), (parts,), jnp.float32, low / len(shards), top_value / len(shards))
        factor_of = factor_of * jnp.repeat(jnp.exp(steps), shape[dim] // parts).reshape((-1,) + (1,) * (len(shape) - 1 - dim))
    return factor_of


def bell_draw(rng, extent, scale, bound, cuts=(), held_as=jnp.bfloat16):
    level = steps_of(rng, extent, cuts, -0.22, 0.18) if cuts else 1.0
    array = jax.random.normal(rng, extent, jnp.float32) * scale * level
    return jnp.minimum(jnp.maximum(array, -bound), bound).astype(held_as)


def setup_inputs(seed: int = 0, part: int = 0) -> dict:
    streams_of = jax.random.split(jax.random.key(seed), 7)
    part_keys = jax.random.split(jax.random.fold_in(streams_of[6], part), 7)
    history = bell_draw(part_keys[0], (HIST, D), 1.0, 6.0, ((0, 16),))
    candidates = bell_draw(part_keys[1], (NC, D), 1.0, 6.0, ((0, 16),))
    hist_length = jax.random.randint(part_keys[2], (1,), HIST // 2, HIST + 1).astype(jnp.int32)
    visible = set_ends(jax.random.randint(part_keys[3], (NC,), 1, HIST + 1), jax.random.fold_in(part_keys[3], 1), 1, HIST).astype(jnp.int32)
    w_proj = bell_draw(streams_of[4], (D, 4 * D), D ** -0.5, 0.1875)
    w_out = bell_draw(streams_of[5], (D, D), D ** -0.5, 0.1875)
    return dict(history=history, candidates=candidates, hist_length=hist_length, visible=visible, w_proj=w_proj, w_out=w_out)


EPS = 1e-06

def layer_norm(rows):
    rows = rows.astype(jnp.float32)
    centred = rows - lax.optimization_barrier(jnp.mean(rows, axis=-1, keepdims=True))
    spread = lax.optimization_barrier(jnp.mean(centred * centred, axis=-1, keepdims=True))
    return centred * lax.rsqrt(spread + EPS)

def attend(query, limit, keys, values):
    rows = query.shape[0]
    n_keys = keys.shape[0]
    head_size = query.shape[1] // HEADS
    q_f = query.astype(jnp.float32).reshape(rows, HEADS, head_size)
    k_f = keys.astype(jnp.float32).reshape(n_keys, HEADS, head_size)
    v_f = values.astype(jnp.float32).reshape(n_keys, HEADS, head_size)
    scores = jnp.einsum('rhd,khd->hrk', q_f, k_f, precision=lax.Precision.HIGHEST)
    position = jnp.arange(n_keys, dtype=jnp.int32)
    seen = (position[None, :] < limit[:, None]).astype(jnp.float32)
    count = (limit + 1).astype(jnp.float32)
    weight = jax.nn.silu(scores * head_size ** (-0.5)) * seen[None] / count[None, :, None]
    weight = weight.astype(jnp.bfloat16).astype(jnp.float32)
    out = jnp.einsum('hrk,khd->rhd', weight, v_f, precision=lax.Precision.HIGHEST)
    return out.reshape(rows, -1)

def reference(history, candidates, hist_length, visible, w_proj, w_out):
    width = w_out.shape[0]
    head_size = width // HEADS
    hist_norm = layer_norm(history).astype(jnp.bfloat16)
    hist_kv = jax.nn.silu(jnp.dot(hist_norm, w_proj[:, 2 * width:], preferred_element_type=jnp.float32)).astype(jnp.bfloat16)
    keys_all = hist_kv[:, :width]
    values_all = hist_kv[:, width:]
    cand_norm = layer_norm(candidates).astype(jnp.bfloat16)
    proj = jax.nn.silu(jnp.dot(cand_norm, w_proj, preferred_element_type=jnp.float32)).astype(jnp.bfloat16)
    gate = proj[:, :width]
    query = proj[:, width:2 * width]
    self_key = proj[:, 2 * width:3 * width]
    self_value = proj[:, 3 * width:]
    limit = jnp.minimum(visible, hist_length[0]).astype(jnp.int32)
    count = (limit + 1).astype(jnp.float32)
    rows_all = query.shape[0]
    blocks = rows_all // C_DEV
    query_blocks = query.reshape(blocks, C_DEV, width)
    limit_blocks = limit.reshape(blocks, C_DEV)

    def one_block(pair):
        return attend(pair[0], pair[1], keys_all, values_all)
    attended = lax.map(one_block, (query_blocks, limit_blocks)).reshape(rows_all, width)
    self_scores = (query.astype(jnp.float32) * self_key.astype(jnp.float32)).reshape(rows_all, HEADS, head_size).sum(-1)
    self_weight = (jax.nn.silu(self_scores * head_size ** (-0.5)) / count[:, None]).astype(jnp.bfloat16).astype(jnp.float32)
    self_term = (self_weight[:, :, None] * self_value.astype(jnp.float32).reshape(rows_all, HEADS, head_size)).reshape(rows_all, width)
    attended = attended + self_term
    mixed = (layer_norm(attended) * gate.astype(jnp.float32)).astype(jnp.bfloat16)
    result = candidates.astype(jnp.float32) + jnp.dot(mixed, w_out, preferred_element_type=jnp.float32)
    return result.astype(jnp.bfloat16)
```

```python
import functools

import jax
import jax.numpy as jnp
from jax import lax
from jax.experimental import pallas as pl
from jax.experimental.pallas import tpu as pltpu
from jax.sharding import PartitionSpec as P

HEADS = 8
EPS = 1e-06
LANES = 128
MESH = pl.DeviceIdType.MESH
F32 = jnp.float32
BF16 = jnp.bfloat16


def layer_norm(rows):
    rows = rows.astype(F32)
    centred = rows - jnp.mean(rows, axis=-1, keepdims=True)
    spread = jnp.mean(centred * centred, axis=-1, keepdims=True)
    return centred * lax.rsqrt(spread + EPS)


def silu(x):
    half = x * 0.5
    return half * jnp.tanh(half) + half


def dot(a, b):
    return jnp.dot(a, b, preferred_element_type=F32)


def kernel(
    n, cols,
    hist_ref, cand_ref, length_ref, visible_ref, w_proj_ref, w_out_ref, out_ref,
    hist, w_kv, w_q, w_gate, w_out, xs, kv, xall, q_all, mask, send_c, recv_c,
    keep, send_d, recv_d, own, load_sem, kv_sem,
    ag_s, ag_r, fw_s, fw_r, rc_s, rc_r, rd_s, rd_r,
):
    chips = n // 2
    me = lax.axis_index("hist")
    chip, side = lax.div(me, 2), lax.rem(me, 2)
    sibling = 2 * chip + (1 - side)
    rows, width = cand_ref.shape
    keys = hist_ref.shape[0]
    half = chips * rows
    head = width // HEADS
    groups = width // cols
    heads_in = cols // head

    def ahead(d):
        return 2 * lax.rem(chip + d, chips) + side

    def behind(d):
        return 2 * lax.rem(chip + chips - d, chips) + side

    load_hist = pltpu.make_async_copy(hist_ref, hist, load_sem.at[0])
    load_hist.start()
    kv_loads = []
    for j in range(2 * groups):
        copy = pltpu.make_async_copy(
            w_proj_ref.at[:, pl.ds(2 * width + j * cols, cols)], w_kv.at[j], kv_sem.at[j]
        )
        copy.start()
        kv_loads.append(copy)
    loads = [
        pltpu.make_async_copy(w_proj_ref.at[:, pl.ds(0, width)], w_gate, load_sem.at[1]),
        pltpu.make_async_copy(w_proj_ref.at[:, pl.ds(width, width)], w_q, load_sem.at[2]),
        pltpu.make_async_copy(w_out_ref, w_out, load_sem.at[3]),
    ]
    for copy in loads:
        copy.start()

    barrier = pltpu.get_barrier_semaphore()
    pl.semaphore_signal(barrier, inc=1, device_id={"hist": sibling}, device_id_type=MESH)
    for d in range(1, chips):
        pl.semaphore_signal(barrier, inc=1, device_id={"hist": ahead(d)}, device_id_type=MESH)

    row = lax.broadcasted_iota(jnp.int32, (rows, LANES), 0)
    lane = lax.broadcasted_iota(jnp.int32, (rows, LANES), 1)
    limit = jnp.zeros((rows, LANES), jnp.int32)
    for r in range(rows):
        limit = jnp.where(row == r, jnp.minimum(visible_ref[r], length_ref[0]), limit)
    count = (limit[:, :1] + 1).astype(F32)
    parts = jnp.where(lane < LANES // 2, limit >> 8, limit & 255)
    cand_norm = layer_norm(cand_ref[...]).astype(BF16)
    xall[0, 0, :, :width] = cand_norm
    xall[0, 0, :, width:] = parts.astype(F32).astype(BF16)
    xs[pl.ds(keys, rows), :] = cand_norm

    pl.semaphore_wait(barrier, chips)

    def remote(src, dst, s, r, to):
        return pltpu.make_async_remote_copy(
            src_ref=src, dst_ref=dst, send_sem=s, recv_sem=r,
            device_id={"hist": to}, device_id_type=MESH,
        )

    gathers = [None] + [
        remote(xall.at[0, 0], xall.at[0, d], ag_s.at[d], ag_r.at[d], ahead(d))
        for d in range(1, chips)
    ]
    forwards = [
        remote(xall.at[0, d], xall.at[1, d], fw_s.at[d], fw_r.at[d], sibling)
        for d in range(chips)
    ]
    for d in range(1, chips):
        gathers[d].start()
    forwards[0].start()

    load_hist.wait()
    for r in range(0, keys, LANES):
        xs[pl.ds(r, LANES), :] = layer_norm(hist[pl.ds(r, LANES), :]).astype(BF16)
    for j in range(2 * groups):
        kv_loads[j].wait()
        kv[j] = silu(dot(xs[...], w_kv[j])).astype(BF16)

    loads[0].wait()
    gate = silu(dot(xs[pl.ds(keys, rows), :], w_gate[...])).astype(BF16).astype(F32)

    def queries(q):
        block = xall[q].reshape(half, width + LANES)
        hi = block[:, width : width + 1].astype(F32)
        lo = block[:, width + LANES // 2 : width + LANES // 2 + 1].astype(F32)
        limits = hi * 256.0 + lo
        position = me * keys + lax.broadcasted_iota(jnp.int32, (half, keys), 1)
        mask[q] = jnp.where(position.astype(F32) < limits, 1.0 / (limits + 1.0), 0.0)
        x = block[:, :width]
        for g in range(groups):
            q_all[q, g] = silu(dot(x, w_q[:, g * cols : (g + 1) * cols])).astype(BF16)

    loads[1].wait()
    for d in range(1, chips):
        gathers[d].wait_recv()
        forwards[d].start()
    queries(0)
    for d in range(chips):
        forwards[d].wait_recv()
    queries(1)

    scale = 0.5 * head ** (-0.5)

    def attend(q, g):
        outs = []
        for h in range(heads_in):
            cut = slice(h * head, (h + 1) * head)
            s = lax.dot_general(
                q_all[q, g, :, cut], kv[g, pl.ds(0, keys), cut],
                (((1,), (1,)), ((), ())), preferred_element_type=F32,
            )
            y = s * scale
            weight = ((y * jnp.tanh(y) + y) * mask[q]).astype(BF16)
            outs.append(dot(weight, kv[groups + g, pl.ds(0, keys), cut]))
        return jnp.concatenate(outs, axis=1)

    crosses, directs = [], []
    shifts = {}

    def shifted(q, g, total):
        if g == 0:
            shifts[q] = jnp.mean(total, axis=-1, keepdims=True)
        return total - shifts[q]

    def pass_on(g):
        crosses[g].wait_recv()
        total = shifted(0, g, keep[g] + recv_c[g].astype(F32))
        own[g] = total[:rows]
        send_d[g] = total.reshape(chips, rows, cols).astype(BF16)
        for d in range(1, chips):
            copy = remote(
                send_d.at[g, d], recv_d.at[g, d], rd_s.at[g, d], rd_r.at[g, d], behind(d)
            )
            copy.start()
            directs.append(copy)

    for g in range(groups):
        send_c[g] = shifted(1, g, attend(1, g)).astype(BF16)
        crosses.append(remote(send_c.at[g], recv_c.at[g], rc_s.at[g], rc_r.at[g], sibling))
        crosses[g].start()
        keep[g] = attend(0, g)
        if g > 0:
            pass_on(g - 1)
    pass_on(groups - 1)

    selves = []
    for g in range(groups):
        q_own = q_all[0, g, :rows, :].astype(F32)
        k_own = kv[g, pl.ds(keys, rows), :].astype(F32)
        v_own = kv[groups + g, pl.ds(keys, rows), :].astype(F32)
        product = q_own * k_own
        for h in range(heads_in):
            cut = slice(h * head, (h + 1) * head)
            s = jnp.sum(product[:, cut], axis=-1, keepdims=True) * (head ** (-0.5))
            weight = (silu(s) / count).astype(BF16).astype(F32)
            selves.append(weight * v_own[:, cut])
    self_term = jnp.concatenate(selves, axis=1)
    loads[2].wait()

    k = 0
    sums = []
    for g in range(groups):
        total = own[g]
        for d in range(1, chips):
            directs[k].wait_recv()
            k += 1
            total = total + recv_d[g, d].astype(F32)
        sums.append(total)
    attended = jnp.concatenate(sums, axis=1) + self_term
    mixed = (layer_norm(attended) * gate).astype(BF16)
    out_ref[...] = (cand_ref[...].astype(F32) + dot(mixed, w_out[...])).astype(BF16)

    for d in range(1, chips):
        gathers[d].wait_send()
    for copy in forwards + crosses + directs:
        copy.wait_send()


def solution(mesh):
    n = mesh.shape["hist"]
    chips = n // 2

    def on_device(history, candidates, hist_length, visible, w_proj, w_out):
        keys = history.shape[0]
        rows, width = candidates.shape
        cols = 2 * (width // HEADS)
        groups = width // cols
        half = chips * rows
        dma = pltpu.SemaphoreType.DMA
        return pl.pallas_call(
            functools.partial(kernel, n, cols),
            out_shape=jax.ShapeDtypeStruct((rows, width), BF16),
            in_specs=[
                pl.BlockSpec(memory_space=pl.ANY),
                pl.BlockSpec(memory_space=pltpu.VMEM),
                pl.BlockSpec(memory_space=pltpu.SMEM),
                pl.BlockSpec(memory_space=pltpu.SMEM),
                pl.BlockSpec(memory_space=pl.ANY),
                pl.BlockSpec(memory_space=pl.ANY),
            ],
            out_specs=pl.BlockSpec(memory_space=pltpu.VMEM),
            scratch_shapes=[
                pltpu.VMEM((keys, width), BF16),
                pltpu.VMEM((2 * groups, width, cols), BF16),
                pltpu.VMEM((width, width), BF16),
                pltpu.VMEM((width, width), BF16),
                pltpu.VMEM((width, width), BF16),
                pltpu.VMEM((keys + rows, width), BF16),
                pltpu.VMEM((2 * groups, keys + rows, cols), BF16),
                pltpu.VMEM((2, chips, rows, width + LANES), BF16),
                pltpu.VMEM((2, groups, half, cols), BF16),
                pltpu.VMEM((2, half, keys), F32),
                pltpu.VMEM((groups, half, cols), BF16),
                pltpu.VMEM((groups, half, cols), BF16),
                pltpu.VMEM((groups, half, cols), F32),
                pltpu.VMEM((groups, chips, rows, cols), BF16),
                pltpu.VMEM((groups, chips, rows, cols), BF16),
                pltpu.VMEM((groups, rows, cols), F32),
                dma((4,)),
                dma((2 * groups,)),
                dma((chips,)),
                dma((chips,)),
                dma((chips,)),
                dma((chips,)),
                dma((groups,)),
                dma((groups,)),
                dma((groups, chips)),
                dma((groups, chips)),
            ],
            compiler_params=pltpu.CompilerParams(
                collective_id=0, has_side_effects=True, vmem_limit_bytes=60 * 1024 * 1024
            ),
            name="score",
        )(history, candidates, hist_length, visible, w_proj, w_out)

    return jax.shard_map(
        on_device,
        mesh=mesh,
        in_specs=(
            P(("groups", "hist"), None),
            P(("groups", "hist"), None),
            P("groups"),
            P(("groups", "hist")),
            P(),
            P(),
        ),
        out_specs=P(("groups", "hist"), None),
        check_vma=False,
    )
```

```python
import functools

import jax
import jax.numpy as jnp
from jax import lax
from jax.experimental import pallas as pl
from jax.experimental.pallas import tpu as pltpu
from jax.sharding import PartitionSpec as P

HEADS = 8
EPS = 1e-06
LANES = 128
MESH = pl.DeviceIdType.MESH
F32 = jnp.float32
BF16 = jnp.bfloat16


def layer_norm(rows):
    rows = rows.astype(F32)
    centred = rows - jnp.mean(rows, axis=-1, keepdims=True)
    spread = jnp.mean(centred * centred, axis=-1, keepdims=True)
    return centred * lax.rsqrt(spread + EPS)


def silu(x):
    half = x * 0.5
    return half * jnp.tanh(half) + half


def dot(a, b):
    return jnp.dot(a, b, preferred_element_type=F32)


def kernel(
    n, cols,
    hist_ref, cand_ref, length_ref, visible_ref, w_proj_ref, w_out_ref, out_ref,
    hist, w_kv, w_q, w_gate, w_out, xs, kv, xall, q_all, mask, send_c, recv_c,
    keep, send_d, recv_d, own, load_sem, kv_sem,
    ag_s, ag_r, fw_s, fw_r, rc_s, rc_r, rd_s, rd_r,
):
    chips = n // 2
    me = lax.axis_index("hist")
    chip, side = lax.div(me, 2), lax.rem(me, 2)
    sibling = 2 * chip + (1 - side)
    rows, width = cand_ref.shape
    keys = hist_ref.shape[0]
    half = chips * rows
    head = width // HEADS
    groups = width // cols
    heads_in = cols // head

    def ahead(d):
        return 2 * lax.rem(chip + d, chips) + side

    def behind(d):
        return 2 * lax.rem(chip + chips - d, chips) + side

    load_hist = pltpu.make_async_copy(hist_ref, hist, load_sem.at[0])
    load_hist.start()
    kv_loads = []
    for j in range(2 * groups):
        copy = pltpu.make_async_copy(
            w_proj_ref.at[:, pl.ds(2 * width + j * cols, cols)], w_kv.at[j], kv_sem.at[j]
        )
        copy.start()
        kv_loads.append(copy)
    loads = [
        pltpu.make_async_copy(w_proj_ref.at[:, pl.ds(0, width)], w_gate, load_sem.at[1]),
        pltpu.make_async_copy(w_proj_ref.at[:, pl.ds(width, width)], w_q, load_sem.at[2]),
        pltpu.make_async_copy(w_out_ref, w_out, load_sem.at[3]),
    ]
    for copy in loads:
        copy.start()

    barrier = pltpu.get_barrier_semaphore()
    pl.semaphore_signal(barrier, inc=1, device_id={"hist": sibling}, device_id_type=MESH)
    for d in range(1, chips):
        pl.semaphore_signal(barrier, inc=1, device_id={"hist": ahead(d)}, device_id_type=MESH)

    row = lax.broadcasted_iota(jnp.int32, (rows, LANES), 0)
    lane = lax.broadcasted_iota(jnp.int32, (rows, LANES), 1)
    limit = jnp.zeros((rows, LANES), jnp.int32)
    for r in range(rows):
        limit = jnp.where(row == r, jnp.minimum(visible_ref[r], length_ref[0]), limit)
    count = (limit[:, :1] + 1).astype(F32)
    parts = jnp.where(lane < LANES // 2, limit >> 8, limit & 255)
    cand_norm = layer_norm(cand_ref[...]).astype(BF16)
    xall[0, 0, :, :width] = cand_norm
    xall[0, 0, :, width:] = parts.astype(F32).astype(BF16)
    xs[pl.ds(keys, rows), :] = cand_norm

    load_hist.wait()
    for r in range(0, keys, LANES):
        xs[pl.ds(r, LANES), :] = layer_norm(hist[pl.ds(r, LANES), :]).astype(BF16)

    pl.semaphore_wait(barrier, chips)

    def remote(src, dst, s, r, to):
        return pltpu.make_async_remote_copy(
            src_ref=src, dst_ref=dst, send_sem=s, recv_sem=r,
            device_id={"hist": to}, device_id_type=MESH,
        )

    gathers = [None] + [
        remote(xall.at[0, 0], xall.at[0, d], ag_s.at[d], ag_r.at[d], ahead(d))
        for d in range(1, chips)
    ]
    forwards = [
        remote(xall.at[0, d], xall.at[1, d], fw_s.at[d], fw_r.at[d], sibling)
        for d in range(chips)
    ]
    for d in range(1, chips):
        gathers[d].start()
    forwards[0].start()

    for j in range(2 * groups):
        kv_loads[j].wait()
        kv[j] = silu(dot(xs[...], w_kv[j])).astype(BF16)

    def limits_of(q):
        block = xall[q].reshape(half, width + LANES)
        hi = block[:, width : width + 1].astype(F32)
        lo = block[:, width + LANES // 2 : width + LANES // 2 + 1].astype(F32)
        limits = hi * 256.0 + lo
        position = me * keys + lax.broadcasted_iota(jnp.int32, (half, keys), 1)
        mask[q] = jnp.where(position.astype(F32) < limits, 1.0 / (limits + 1.0), 0.0)

    def query(q, g):
        x = xall[q, :, :, :width].reshape(half, width)
        q_all[q, g] = silu(dot(x, w_q[:, g * cols : (g + 1) * cols])).astype(BF16)

    loads[1].wait()
    for d in range(1, chips):
        gathers[d].wait_recv()
        forwards[d].start()
    limits_of(0)

    scale = 0.5 * head ** (-0.5)

    def attend(q, g):
        outs = []
        for h in range(heads_in):
            cut = slice(h * head, (h + 1) * head)
            s = lax.dot_general(
                q_all[q, g, :, cut], kv[g, pl.ds(0, keys), cut],
                (((1,), (1,)), ((), ())), preferred_element_type=F32,
            )
            y = s * scale
            weight = ((y * jnp.tanh(y) + y) * mask[q]).astype(BF16)
            outs.append(dot(weight, kv[groups + g, pl.ds(0, keys), cut]))
        return jnp.concatenate(outs, axis=1)

    crosses, directs = [], []
    shifts = []

    def pass_on(g):
        crosses[g].wait_recv()
        total = keep[g] + recv_c[g]
        if g == 0:
            shifts.append(jnp.mean(total, axis=-1, keepdims=True))
        total = total - shifts[0]
        own[g] = total[:rows]
        send_d[g] = total.reshape(chips, rows, cols).astype(BF16)
        for d in range(1, chips):
            copy = remote(
                send_d.at[g, d], recv_d.at[g, d], rd_s.at[g, d], rd_r.at[g, d], behind(d)
            )
            copy.start()
            directs.append(copy)

    query(0, 0)
    keep[0] = attend(0, 0)
    loads[0].wait()
    gate = silu(dot(xs[pl.ds(keys, rows), :], w_gate[...])).astype(BF16).astype(F32)
    for d in range(chips):
        forwards[d].wait_recv()
    limits_of(1)
    for g in range(groups):
        query(1, g)
        send_c[g] = attend(1, g)
        crosses.append(remote(send_c.at[g], recv_c.at[g], rc_s.at[g], rc_r.at[g], sibling))
        crosses[g].start()
        if g + 1 < groups:
            query(0, g + 1)
            keep[g + 1] = attend(0, g + 1)
        if g > 0:
            pass_on(g - 1)
    pass_on(groups - 1)

    selves = []
    for g in range(groups):
        q_own = q_all[0, g, :rows, :].astype(F32)
        k_own = kv[g, pl.ds(keys, rows), :].astype(F32)
        v_own = kv[groups + g, pl.ds(keys, rows), :].astype(F32)
        product = q_own * k_own
        for h in range(heads_in):
            cut = slice(h * head, (h + 1) * head)
            s = jnp.sum(product[:, cut], axis=-1, keepdims=True) * (head ** (-0.5))
            weight = (silu(s) / count).astype(BF16).astype(F32)
            selves.append(weight * v_own[:, cut])
    self_term = jnp.concatenate(selves, axis=1)
    loads[2].wait()

    k = 0
    sums = []
    for g in range(groups):
        total = own[g]
        for d in range(1, chips):
            directs[k].wait_recv()
            k += 1
            total = total + recv_d[g, d].astype(F32)
        sums.append(total)
    attended = jnp.concatenate(sums, axis=1) + self_term
    mixed = (layer_norm(attended) * gate).astype(BF16)
    out_ref[...] = (cand_ref[...].astype(F32) + dot(mixed, w_out[...])).astype(BF16)

    for d in range(1, chips):
        gathers[d].wait_send()
    for copy in forwards + crosses + directs:
        copy.wait_send()


def solution(mesh):
    n = mesh.shape["hist"]
    chips = n // 2

    def on_device(history, candidates, hist_length, visible, w_proj, w_out):
        keys = history.shape[0]
        rows, width = candidates.shape
        cols = 2 * (width // HEADS)
        groups = width // cols
        half = chips * rows
        dma = pltpu.SemaphoreType.DMA
        return pl.pallas_call(
            functools.partial(kernel, n, cols),
            out_shape=jax.ShapeDtypeStruct((rows, width), BF16),
            in_specs=[
                pl.BlockSpec(memory_space=pl.ANY),
                pl.BlockSpec(memory_space=pltpu.VMEM),
                pl.BlockSpec(memory_space=pltpu.SMEM),
                pl.BlockSpec(memory_space=pltpu.SMEM),
                pl.BlockSpec(memory_space=pl.ANY),
                pl.BlockSpec(memory_space=pl.ANY),
            ],
            out_specs=pl.BlockSpec(memory_space=pltpu.VMEM),
            scratch_shapes=[
                pltpu.VMEM((keys, width), BF16),
                pltpu.VMEM((2 * groups, width, cols), BF16),
                pltpu.VMEM((width, width), BF16),
                pltpu.VMEM((width, width), BF16),
                pltpu.VMEM((width, width), BF16),
                pltpu.VMEM((keys + rows, width), BF16),
                pltpu.VMEM((2 * groups, keys + rows, cols), BF16),
                pltpu.VMEM((2, chips, rows, width + LANES), BF16),
                pltpu.VMEM((2, groups, half, cols), BF16),
                pltpu.VMEM((2, half, keys), F32),
                pltpu.VMEM((groups, half, cols), F32),
                pltpu.VMEM((groups, half, cols), F32),
                pltpu.VMEM((groups, half, cols), F32),
                pltpu.VMEM((groups, chips, rows, cols), BF16),
                pltpu.VMEM((groups, chips, rows, cols), BF16),
                pltpu.VMEM((groups, rows, cols), F32),
                dma((4,)),
                dma((2 * groups,)),
                dma((chips,)),
                dma((chips,)),
                dma((chips,)),
                dma((chips,)),
                dma((groups,)),
                dma((groups,)),
                dma((groups, chips)),
                dma((groups, chips)),
            ],
            compiler_params=pltpu.CompilerParams(
                collective_id=0, has_side_effects=True, vmem_limit_bytes=60 * 1024 * 1024
            ),
            name="score",
        )(history, candidates, hist_length, visible, w_proj, w_out)

    return jax.shard_map(
        on_device,
        mesh=mesh,
        in_specs=(
            P(("groups", "hist"), None),
            P(("groups", "hist"), None),
            P("groups"),
            P(("groups", "hist")),
            P(),
            P(),
        ),
        out_specs=P(("groups", "hist"), None),
        check_vma=False,
    )
```

```python
import functools

import jax
import jax.numpy as jnp
from jax import lax
from jax.experimental import pallas as pl
from jax.experimental.pallas import tpu as pltpu
from jax.sharding import PartitionSpec as P

HEADS = 8
EPS = 1e-06
LANES = 128
MESH = pl.DeviceIdType.MESH
F32 = jnp.float32
BF16 = jnp.bfloat16


def layer_norm(rows):
    rows = rows.astype(F32)
    centred = rows - jnp.mean(rows, axis=-1, keepdims=True)
    spread = jnp.mean(centred * centred, axis=-1, keepdims=True)
    return centred * lax.rsqrt(spread + EPS)


def silu(x):
    half = x * 0.5
    return half * jnp.tanh(half) + half


def dot(a, b):
    return jnp.dot(a, b, preferred_element_type=F32)


def kernel(
    n, cols,
    hist_ref, cand_ref, length_ref, visible_ref, w_proj_ref, w_out_ref, out_ref,
    hist, w_kv, w_q, w_gate, w_out, xs, kv, xall, q_all, mask, send_c, recv_c,
    keep, send_d, recv_d, own, load_sem, kv_sem,
    ag_s, ag_r, fw_s, fw_r, rc_s, rc_r, rd_s, rd_r,
):
    chips = n // 2
    me = lax.axis_index("hist")
    chip, side = lax.div(me, 2), lax.rem(me, 2)
    sibling = 2 * chip + (1 - side)
    rows, width = cand_ref.shape
    keys = hist_ref.shape[0]
    half = chips * rows
    head = width // HEADS
    groups = width // cols
    heads_in = cols // head

    def ahead(d):
        return 2 * lax.rem(chip + d, chips) + side

    def behind(d):
        return 2 * lax.rem(chip + chips - d, chips) + side

    load_hist = pltpu.make_async_copy(hist_ref, hist, load_sem.at[0])
    load_hist.start()
    kv_loads = []
    for j in range(2 * groups):
        copy = pltpu.make_async_copy(
            w_proj_ref.at[:, pl.ds(2 * width + j * cols, cols)], w_kv.at[j], kv_sem.at[j]
        )
        copy.start()
        kv_loads.append(copy)
    loads = [
        pltpu.make_async_copy(w_proj_ref.at[:, pl.ds(0, width)], w_gate, load_sem.at[1]),
        pltpu.make_async_copy(w_proj_ref.at[:, pl.ds(width, width)], w_q, load_sem.at[2]),
        pltpu.make_async_copy(w_out_ref, w_out, load_sem.at[3]),
    ]
    for copy in loads:
        copy.start()

    barrier = pltpu.get_barrier_semaphore()
    pl.semaphore_signal(barrier, inc=1, device_id={"hist": sibling}, device_id_type=MESH)
    for d in range(1, chips):
        pl.semaphore_signal(barrier, inc=1, device_id={"hist": ahead(d)}, device_id_type=MESH)

    row = lax.broadcasted_iota(jnp.int32, (rows, LANES), 0)
    lane = lax.broadcasted_iota(jnp.int32, (rows, LANES), 1)
    limit = jnp.zeros((rows, LANES), jnp.int32)
    for r in range(rows):
        limit = jnp.where(row == r, jnp.minimum(visible_ref[r], length_ref[0]), limit)
    count = (limit[:, :1] + 1).astype(F32)
    parts = jnp.where(lane < LANES // 2, limit >> 8, limit & 255)
    cand_norm = layer_norm(cand_ref[...]).astype(BF16)
    xall[0, 0, :, :width] = cand_norm
    xall[0, 0, :, width:] = parts.astype(F32).astype(BF16)
    xs[pl.ds(keys, rows), :] = cand_norm

    pl.semaphore_wait(barrier, chips)

    def remote(src, dst, s, r, to):
        return pltpu.make_async_remote_copy(
            src_ref=src, dst_ref=dst, send_sem=s, recv_sem=r,
            device_id={"hist": to}, device_id_type=MESH,
        )

    order = sorted(range(1, chips), key=lambda d: abs(d - chips // 2))
    gathers = [None] + [
        remote(xall.at[0, 0], xall.at[0, d], ag_s.at[d], ag_r.at[d], ahead(d))
        for d in range(1, chips)
    ]
    forwards = [
        remote(xall.at[0, d], xall.at[1, d], fw_s.at[d], fw_r.at[d], sibling)
        for d in range(chips)
    ]
    for d in order:
        gathers[d].start()
    forwards[0].start()

    load_hist.wait()
    for r in range(0, keys, LANES):
        xs[pl.ds(r, LANES), :] = layer_norm(hist[pl.ds(r, LANES), :]).astype(BF16)
    for j in range(2 * groups):
        kv_loads[j].wait()
        kv[j] = silu(dot(xs[...], w_kv[j])).astype(BF16)

    loads[0].wait()
    gate = silu(dot(xs[pl.ds(keys, rows), :], w_gate[...])).astype(BF16).astype(F32)

    def queries(q):
        block = xall[q].reshape(half, width + LANES)
        hi = block[:, width : width + 1].astype(F32)
        lo = block[:, width + LANES // 2 : width + LANES // 2 + 1].astype(F32)
        limits = hi * 256.0 + lo
        position = me * keys + lax.broadcasted_iota(jnp.int32, (half, keys), 1)
        mask[q] = jnp.where(position.astype(F32) < limits, 1.0 / (limits + 1.0), 0.0)
        x = block[:, :width]
        for g in range(groups):
            q_all[q, g] = silu(dot(x, w_q[:, g * cols : (g + 1) * cols])).astype(BF16)

    loads[1].wait()
    for d in range(1, chips):
        gathers[d].wait_recv()
        forwards[d].start()
    queries(0)
    for d in range(chips):
        forwards[d].wait_recv()
    queries(1)

    scale = 0.5 * head ** (-0.5)

    def attend(q, g):
        outs = []
        for h in range(heads_in):
            cut = slice(h * head, (h + 1) * head)
            s = lax.dot_general(
                q_all[q, g, :, cut], kv[g, pl.ds(0, keys), cut],
                (((1,), (1,)), ((), ())), preferred_element_type=F32,
            )
            y = s * scale
            weight = ((y * jnp.tanh(y) + y) * mask[q]).astype(BF16)
            outs.append(dot(weight, kv[groups + g, pl.ds(0, keys), cut]))
        return jnp.concatenate(outs, axis=1)

    crosses, directs = [], []
    shifts = []

    def pass_on(g):
        crosses[g].wait_recv()
        total = keep[g] + recv_c[g]
        if g == 0:
            shifts.append(jnp.mean(total, axis=-1, keepdims=True))
        total = total - shifts[0]
        own[g] = total[:rows]
        send_d[g] = total.reshape(chips, rows, cols).astype(BF16)
        for d in order:
            copy = remote(
                send_d.at[g, d], recv_d.at[g, d], rd_s.at[g, d], rd_r.at[g, d], behind(d)
            )
            copy.start()
            directs.append(copy)

    for g in range(groups):
        send_c[g] = attend(1, g)
        crosses.append(remote(send_c.at[g], recv_c.at[g], rc_s.at[g], rc_r.at[g], sibling))
        crosses[g].start()
        keep[g] = attend(0, g)
        if g > 0:
            pass_on(g - 1)
    pass_on(groups - 1)

    selves = []
    for g in range(groups):
        q_own = q_all[0, g, :rows, :].astype(F32)
        k_own = kv[g, pl.ds(keys, rows), :].astype(F32)
        v_own = kv[groups + g, pl.ds(keys, rows), :].astype(F32)
        product = q_own * k_own
        for h in range(heads_in):
            cut = slice(h * head, (h + 1) * head)
            s = jnp.sum(product[:, cut], axis=-1, keepdims=True) * (head ** (-0.5))
            weight = (silu(s) / count).astype(BF16).astype(F32)
            selves.append(weight * v_own[:, cut])
    self_term = jnp.concatenate(selves, axis=1)
    loads[2].wait()

    k = 0
    sums = []
    for g in range(groups):
        total = own[g]
        for d in order:
            directs[k].wait_recv()
            k += 1
            total = total + recv_d[g, d].astype(F32)
        sums.append(total)
    attended = jnp.concatenate(sums, axis=1) + self_term
    mixed = (layer_norm(attended) * gate).astype(BF16)
    out_ref[...] = (cand_ref[...].astype(F32) + dot(mixed, w_out[...])).astype(BF16)

    for d in range(1, chips):
        gathers[d].wait_send()
    for copy in forwards + crosses + directs:
        copy.wait_send()


def solution(mesh):
    n = mesh.shape["hist"]
    chips = n // 2

    def on_device(history, candidates, hist_length, visible, w_proj, w_out):
        keys = history.shape[0]
        rows, width = candidates.shape
        cols = 2 * (width // HEADS)
        groups = width // cols
        half = chips * rows
        dma = pltpu.SemaphoreType.DMA
        return pl.pallas_call(
            functools.partial(kernel, n, cols),
            out_shape=jax.ShapeDtypeStruct((rows, width), BF16),
            in_specs=[
                pl.BlockSpec(memory_space=pl.ANY),
                pl.BlockSpec(memory_space=pltpu.VMEM),
                pl.BlockSpec(memory_space=pltpu.SMEM),
                pl.BlockSpec(memory_space=pltpu.SMEM),
                pl.BlockSpec(memory_space=pl.ANY),
                pl.BlockSpec(memory_space=pl.ANY),
            ],
            out_specs=pl.BlockSpec(memory_space=pltpu.VMEM),
            scratch_shapes=[
                pltpu.VMEM((keys, width), BF16),
                pltpu.VMEM((2 * groups, width, cols), BF16),
                pltpu.VMEM((width, width), BF16),
                pltpu.VMEM((width, width), BF16),
                pltpu.VMEM((width, width), BF16),
                pltpu.VMEM((keys + rows, width), BF16),
                pltpu.VMEM((2 * groups, keys + rows, cols), BF16),
                pltpu.VMEM((2, chips, rows, width + LANES), BF16),
                pltpu.VMEM((2, groups, half, cols), BF16),
                pltpu.VMEM((2, half, keys), F32),
                pltpu.VMEM((groups, half, cols), F32),
                pltpu.VMEM((groups, half, cols), F32),
                pltpu.VMEM((groups, half, cols), F32),
                pltpu.VMEM((groups, chips, rows, cols), BF16),
                pltpu.VMEM((groups, chips, rows, cols), BF16),
                pltpu.VMEM((groups, rows, cols), F32),
                dma((4,)),
                dma((2 * groups,)),
                dma((chips,)),
                dma((chips,)),
                dma((chips,)),
                dma((chips,)),
                dma((groups,)),
                dma((groups,)),
                dma((groups, chips)),
                dma((groups, chips)),
            ],
            compiler_params=pltpu.CompilerParams(
                collective_id=0, has_side_effects=True, vmem_limit_bytes=60 * 1024 * 1024
            ),
            name="score",
        )(history, candidates, hist_length, visible, w_proj, w_out)

    return jax.shard_map(
        on_device,
        mesh=mesh,
        in_specs=(
            P(("groups", "hist"), None),
            P(("groups", "hist"), None),
            P("groups"),
            P(("groups", "hist")),
            P(),
            P(),
        ),
        out_specs=P(("groups", "hist"), None),
        check_vma=False,
    )
```

```python
import functools

import jax
import jax.numpy as jnp
from jax import lax
from jax.experimental import pallas as pl
from jax.experimental.pallas import tpu as pltpu
from jax.sharding import PartitionSpec as P

HEADS = 8
EPS = 1e-06
LANES = 128
MESH = pl.DeviceIdType.MESH
F32 = jnp.float32
BF16 = jnp.bfloat16


def layer_norm(rows):
    rows = rows.astype(F32)
    centred = rows - jnp.mean(rows, axis=-1, keepdims=True)
    spread = jnp.mean(centred * centred, axis=-1, keepdims=True)
    return centred * lax.rsqrt(spread + EPS)


def silu(x):
    half = x * 0.5
    return half * jnp.tanh(half) + half


def dot(a, b):
    return jnp.dot(a, b, preferred_element_type=F32)


def kernel(
    n, cols,
    hist_ref, cand_ref, length_ref, visible_ref, w_proj_ref, w_out_ref, out_ref,
    hist, w_kv, w_q, w_gate, w_out, xs, kv, xall, q_all, mask, send_c, recv_c,
    keep, send_d, recv_d, own, load_sem, kv_sem,
    ag_s, ag_r, fw_s, fw_r, rc_s, rc_r, rd_s, rd_r,
):
    chips = n // 2
    me = lax.axis_index("hist")
    chip, side = lax.div(me, 2), lax.rem(me, 2)
    sibling = 2 * chip + (1 - side)
    rows, width = cand_ref.shape
    keys = hist_ref.shape[0]
    half = chips * rows
    head = width // HEADS
    groups = width // cols
    heads_in = cols // head

    def ahead(d):
        return 2 * lax.rem(chip + d, chips) + side

    def behind(d):
        return 2 * lax.rem(chip + chips - d, chips) + side

    load_hist = pltpu.make_async_copy(hist_ref, hist, load_sem.at[0])
    load_hist.start()
    kv_loads = []
    for j in range(2 * groups):
        copy = pltpu.make_async_copy(
            w_proj_ref.at[:, pl.ds(2 * width + j * cols, cols)], w_kv.at[j], kv_sem.at[j]
        )
        copy.start()
        kv_loads.append(copy)
    loads = [
        pltpu.make_async_copy(w_proj_ref.at[:, pl.ds(0, width)], w_gate, load_sem.at[1]),
        pltpu.make_async_copy(w_proj_ref.at[:, pl.ds(width, width)], w_q, load_sem.at[2]),
        pltpu.make_async_copy(w_out_ref, w_out, load_sem.at[3]),
    ]
    for copy in loads:
        copy.start()

    barrier = pltpu.get_barrier_semaphore()
    pl.semaphore_signal(barrier, inc=1, device_id={"hist": sibling}, device_id_type=MESH)
    for d in range(1, chips):
        pl.semaphore_signal(barrier, inc=1, device_id={"hist": ahead(d)}, device_id_type=MESH)

    row = lax.broadcasted_iota(jnp.int32, (rows, LANES), 0)
    lane = lax.broadcasted_iota(jnp.int32, (rows, LANES), 1)
    limit = jnp.zeros((rows, LANES), jnp.int32)
    for r in range(rows):
        limit = jnp.where(row == r, jnp.minimum(visible_ref[r], length_ref[0]), limit)
    count = (limit[:, :1] + 1).astype(F32)
    parts = jnp.where(lane < LANES // 2, limit >> 8, limit & 255)
    cand_norm = layer_norm(cand_ref[...]).astype(BF16)
    xall[0, 0, :, :width] = cand_norm
    xall[0, 0, :, width:] = parts.astype(F32).astype(BF16)
    xs[pl.ds(keys, rows), :] = cand_norm

    pl.semaphore_wait(barrier, chips)

    def remote(src, dst, s, r, to):
        return pltpu.make_async_remote_copy(
            src_ref=src, dst_ref=dst, send_sem=s, recv_sem=r,
            device_id={"hist": to}, device_id_type=MESH,
        )

    order = sorted(range(1, chips), key=lambda d: abs(d - chips // 2))
    gathers = [None] + [
        remote(xall.at[0, 0], xall.at[0, d], ag_s.at[d], ag_r.at[d], ahead(d))
        for d in range(1, chips)
    ]
    forwards = [
        remote(xall.at[0, d], xall.at[1, d], fw_s.at[d], fw_r.at[d], sibling)
        for d in range(chips)
    ]
    for d in order:
        gathers[d].start()
    forwards[0].start()

    load_hist.wait()
    for r in range(0, keys, LANES):
        xs[pl.ds(r, LANES), :] = layer_norm(hist[pl.ds(r, LANES), :]).astype(BF16)
    for j in range(2 * groups):
        kv_loads[j].wait()
        kv[j] = silu(dot(xs[...], w_kv[j])).astype(BF16)

    loads[0].wait()
    gate = silu(dot(xs[pl.ds(keys, rows), :], w_gate[...])).astype(BF16).astype(F32)

    def queries(q):
        block = xall[q].reshape(half, width + LANES)
        hi = block[:, width : width + 1].astype(F32)
        lo = block[:, width + LANES // 2 : width + LANES // 2 + 1].astype(F32)
        limits = hi * 256.0 + lo
        position = me * keys + lax.broadcasted_iota(jnp.int32, (half, keys), 1)
        mask[q] = jnp.where(position.astype(F32) < limits, 1.0 / (limits + 1.0), 0.0)
        x = block[:, :width]
        for g in range(groups):
            q_all[q, g] = silu(dot(x, w_q[:, g * cols : (g + 1) * cols])).astype(BF16)

    loads[1].wait()
    for d in range(1, chips):
        gathers[d].wait_recv()
        forwards[d].start()
    queries(0)
    for d in range(chips):
        forwards[d].wait_recv()
    queries(1)

    scale = 0.5 * head ** (-0.5)

    def attend(q, g):
        outs = []
        for h in range(heads_in):
            cut = slice(h * head, (h + 1) * head)
            s = lax.dot_general(
                q_all[q, g, :, cut], kv[g, pl.ds(0, keys), cut],
                (((1,), (1,)), ((), ())), preferred_element_type=F32,
            )
            y = s * scale
            weight = ((y * jnp.tanh(y) + y) * mask[q]).astype(BF16)
            outs.append(dot(weight, kv[groups + g, pl.ds(0, keys), cut]))
        return jnp.concatenate(outs, axis=1)

    crosses, directs = [], []

    def pass_on(g):
        crosses[g].wait_recv()
        total = keep[g] + recv_c[g]
        own[g] = total[:rows]
        send_d[g] = total.reshape(chips, rows, cols)
        for d in order:
            copy = remote(
                send_d.at[g, d], recv_d.at[g, d], rd_s.at[g, d], rd_r.at[g, d], behind(d)
            )
            copy.start()
            directs.append(copy)

    for g in range(groups):
        send_c[g] = attend(1, g)
        crosses.append(remote(send_c.at[g], recv_c.at[g], rc_s.at[g], rc_r.at[g], sibling))
        crosses[g].start()
        keep[g] = attend(0, g)
        if g > 0:
            pass_on(g - 1)
    pass_on(groups - 1)

    selves = []
    for g in range(groups):
        q_own = q_all[0, g, :rows, :].astype(F32)
        k_own = kv[g, pl.ds(keys, rows), :].astype(F32)
        v_own = kv[groups + g, pl.ds(keys, rows), :].astype(F32)
        product = q_own * k_own
        for h in range(heads_in):
            cut = slice(h * head, (h + 1) * head)
            s = jnp.sum(product[:, cut], axis=-1, keepdims=True) * (head ** (-0.5))
            weight = (silu(s) / count).astype(BF16).astype(F32)
            selves.append(weight * v_own[:, cut])
    self_term = jnp.concatenate(selves, axis=1)
    loads[2].wait()

    k = 0
    sums = []
    for g in range(groups):
        total = own[g]
        for d in order:
            directs[k].wait_recv()
            k += 1
            total = total + recv_d[g, d]
        sums.append(total)
    attended = jnp.concatenate(sums, axis=1) + self_term
    mixed = (layer_norm(attended) * gate).astype(BF16)
    out_ref[...] = (cand_ref[...].astype(F32) + dot(mixed, w_out[...])).astype(BF16)

    for d in range(1, chips):
        gathers[d].wait_send()
    for copy in forwards + crosses + directs:
        copy.wait_send()


def solution(mesh):
    n = mesh.shape["hist"]
    chips = n // 2

    def on_device(history, candidates, hist_length, visible, w_proj, w_out):
        keys = history.shape[0]
        rows, width = candidates.shape
        cols = 2 * (width // HEADS)
        groups = width // cols
        half = chips * rows
        dma = pltpu.SemaphoreType.DMA
        return pl.pallas_call(
            functools.partial(kernel, n, cols),
            out_shape=jax.ShapeDtypeStruct((rows, width), BF16),
            in_specs=[
                pl.BlockSpec(memory_space=pl.ANY),
                pl.BlockSpec(memory_space=pltpu.VMEM),
                pl.BlockSpec(memory_space=pltpu.SMEM),
                pl.BlockSpec(memory_space=pltpu.SMEM),
                pl.BlockSpec(memory_space=pl.ANY),
                pl.BlockSpec(memory_space=pl.ANY),
            ],
            out_specs=pl.BlockSpec(memory_space=pltpu.VMEM),
            scratch_shapes=[
                pltpu.VMEM((keys, width), BF16),
                pltpu.VMEM((2 * groups, width, cols), BF16),
                pltpu.VMEM((width, width), BF16),
                pltpu.VMEM((width, width), BF16),
                pltpu.VMEM((width, width), BF16),
                pltpu.VMEM((keys + rows, width), BF16),
                pltpu.VMEM((2 * groups, keys + rows, cols), BF16),
                pltpu.VMEM((2, chips, rows, width + LANES), BF16),
                pltpu.VMEM((2, groups, half, cols), BF16),
                pltpu.VMEM((2, half, keys), F32),
                pltpu.VMEM((groups, half, cols), F32),
                pltpu.VMEM((groups, half, cols), F32),
                pltpu.VMEM((groups, half, cols), F32),
                pltpu.VMEM((groups, chips, rows, cols), F32),
                pltpu.VMEM((groups, chips, rows, cols), F32),
                pltpu.VMEM((groups, rows, cols), F32),
                dma((4,)),
                dma((2 * groups,)),
                dma((chips,)),
                dma((chips,)),
                dma((chips,)),
                dma((chips,)),
                dma((groups,)),
                dma((groups,)),
                dma((groups, chips)),
                dma((groups, chips)),
            ],
            compiler_params=pltpu.CompilerParams(
                collective_id=0, has_side_effects=True, vmem_limit_bytes=60 * 1024 * 1024
            ),
            name="score",
        )(history, candidates, hist_length, visible, w_proj, w_out)

    return jax.shard_map(
        on_device,
        mesh=mesh,
        in_specs=(
            P(("groups", "hist"), None),
            P(("groups", "hist"), None),
            P("groups"),
            P(("groups", "hist")),
            P(),
            P(),
        ),
        out_specs=P(("groups", "hist"), None),
        check_vma=False,
    )
```
